32 devices in a mesh: gx: 8 (over z, core), gy: 4 (over y, x).
Axes of the slice: x: 2, y: 2, z: 4, core: 2. Of those that a mesh axis runs over, the one named last changes fastest.
Arguments:
- fine_velocity: float32 [3, 64, 32, 128], P(None, 'gx', 'gy'), may hold values from -6 to 6
- fine_stress: float32 [6, 64, 32, 128], P(None, 'gx', 'gy'), may hold values from -6 to 6
- fine_memory: float32 [3, 6, 64, 32, 128], P(None, None, 'gx', 'gy'), may hold values from -1.8 to 1.8
- fine_buoyancy: float32 [64, 32, 128], P('gx', 'gy'), may hold values from 0.5 to 2
- fine_moduli: float32 [2, 64, 32, 128], P(None, 'gx', 'gy'), may hold values from 0.4 to 1.6
- fine_anelastic: float32 [2, 3, 64, 32, 128], P(None, None, 'gx', 'gy'), may hold values from 0.05 to 0.5
- fine_slopes: float32 [2, 64, 32, 128], P(None, 'gx', 'gy'), may hold values from -0.4 to 0.4
- fine_stretch: float32 [64, 32, 128], P('gx', 'gy'), may hold values from 0.7 to 1.4
- coarse_velocity: float32 [3, 32, 16, 128], P(None, 'gx', 'gy'), may hold values from -6 to 6
- coarse_stress: float32 [6, 32, 16, 128], P(None, 'gx', 'gy'), may hold values from -6 to 6
- coarse_memory: float32 [3, 6, 32, 16, 128], P(None, None, 'gx', 'gy'), may hold values from -1.8 to 1.8
- coarse_buoyancy: float32 [32, 16, 128], P('gx', 'gy'), may hold values from 0.5 to 2
- coarse_moduli: float32 [2, 32, 16, 128], P(None, 'gx', 'gy'), may hold values from 0.4 to 1.6
- coarse_anelastic: float32 [2, 3, 32, 16, 128], P(None, None, 'gx', 'gy'), may hold values from 0.05 to 0.5
- relax_rates: float32 [3], replicated, may hold values from 0.05 to 1
Outputs:
- new_fine_velocity: float32 [3, 64, 32, 128], P(None, 'gx', 'gy')
- new_fine_stress: float32 [6, 64, 32, 128], P(None, 'gx', 'gy')
- new_fine_memory: float32 [3, 6, 64, 32, 128], P(None, None, 'gx', 'gy')
- new_coarse_velocity: float32 [3, 32, 16, 128], P(None, 'gx', 'gy')
- new_coarse_stress: float32 [6, 32, 16, 128], P(None, 'gx', 'gy')
- new_coarse_memory: float32 [3, 6, 32, 16, 128], P(None, None, 'gx', 'gy')
The draws below stay inside these ranges and needn't reach their ends.
All inputs are finite; a program needn't handle non-finite values.
Results may differ from the reference program's by a relative error of at most 0.00002.
Values sent between devices are 32-bit elements; how exact they have to be, the bound alone decides.
No kernel may reach another device: no remote copies, remote signals or barrier semaphores. Data moves between devices by JAX's collectives and lax.ppermute only.
A program may use at most 64 MiB of HBM per device.

```python
import math
import jax
import jax.numpy as jnp
from jax import lax

FZ = 128
KZ = 128
MECH = 3
NX = 64
NY = 32
MX = 32
MY = 16


def block_scale(rng, shape, cuts, smallest, top_value):
    loudness = 1.0
    for position, blocks in cuts:
        steps = jax.random.uniform(jax.random.fold_in(jax.random.fold_in(rng, 6), position), (blocks,), jnp.float32, smallest / len(cuts), top_value / len(cuts))
        loudness = loudness * jnp.repeat(jnp.exp(steps), shape[position] // blocks).reshape((-1,) + (1,) * (len(shape) - 1 - position))
    return loudness


def scatter_about(rng, dims, scale, most, cuts=(), kind=jnp.bfloat16):
    drawn = scale * jax.random.normal(rng, dims, jnp.float32)
    if cuts:
        drawn = drawn * block_scale(rng, dims, cuts, -0.22, 0.18)
    return jnp.clip(drawn, -most, most).astype(kind)


def setup_inputs(seed: int = 0) -> dict:
    keys = jax.random.split(jax.random.key(seed), 16)
    return {
        "fine_velocity": scatter_about(keys[0], (3, NX, NY, FZ), 1.0, 6.0, ((1, 8), (2, 4)), jnp.float32),
        "fine_stress": scatter_about(keys[1], (6, NX, NY, FZ), 1.0, 6.0, ((1, 8), (2, 4)), jnp.float32),
        "fine_memory": scatter_about(keys[2], (MECH, 6, NX, NY, FZ), 0.3, 1.8, ((2, 8), (3, 4)), jnp.float32),
        "fine_buoyancy": jnp.clip(jnp.exp(math.log(2.0) - 1.3862944 * jax.random.uniform(keys[3], (NX, NY, FZ), jnp.float32) ** block_scale(keys[3], (NX, NY, FZ), ((0, 8), (1, 4)), -0.2, 0.2)), 0.5, 2.0),
        "fine_moduli": jnp.clip(0.4 + 1.2 * jax.random.uniform(keys[4], (2, NX, NY, FZ), jnp.float32) ** block_scale(keys[4], (2, NX, NY, FZ), ((1, 8), (2, 4)), -0.2, 0.2), 0.4, 1.6),
        "fine_anelastic": jnp.clip(0.05 + 0.45 * jax.random.uniform(keys[5], (2, MECH, NX, NY, FZ), jnp.float32) ** block_scale(keys[5], (2, MECH, NX, NY, FZ), ((2, 8), (3, 4)), -0.2, 0.2), 0.05, 0.5),
        "fine_slopes": jnp.clip(jax.random.uniform(keys[6], (2, NX, NY, FZ), jnp.float32, -0.4, 0.4) * block_scale(keys[6], (2, NX, NY, FZ), ((1, 8), (2, 4)), -0.4, 0.0), -0.4, 0.4),
        "fine_stretch": jnp.clip(jnp.exp(math.log(1.4) - 0.6931472 * jax.random.uniform(keys[7], (NX, NY, FZ), jnp.float32) ** block_scale(keys[7], (NX, NY, FZ), ((0, 8), (1, 4)), -0.2, 0.2)), 0.7, 1.4),
        "coarse_velocity": scatter_about(keys[8], (3, MX, MY, KZ), 1.0, 6.0, ((1, 8), (2, 4)), jnp.float32),
        "coarse_stress": scatter_about(keys[9], (6, MX, MY, KZ), 1.0, 6.0, ((1, 8), (2, 4)), jnp.float32),
        "coarse_memory": scatter_about(keys[10], (MECH, 6, MX, MY, KZ), 0.3, 1.8, ((2, 8), (3, 4)), jnp.float32),
        "coarse_buoyancy": jnp.clip(jnp.exp(math.log(2.0) - 1.3862944 * jax.random.uniform(keys[11], (MX, MY, KZ), jnp.float32) ** block_scale(keys[11], (MX, MY, KZ), ((0, 8), (1, 4)), -0.2, 0.2)), 0.5, 2.0),
        "coarse_moduli": jnp.clip(0.4 + 1.2 * jax.random.uniform(keys[12], (2, MX, MY, KZ), jnp.float32) ** block_scale(keys[12], (2, MX, MY, KZ), ((1, 8), (2, 4)), -0.2, 0.2), 0.4, 1.6),
        "coarse_anelastic": jnp.clip(0.05 + 0.45 * jax.random.uniform(keys[13], (2, MECH, MX, MY, KZ), jnp.float32) ** block_scale(keys[13], (2, MECH, MX, MY, KZ), ((2, 8), (3, 4)), -0.2, 0.2), 0.05, 0.5),
        "relax_rates": jnp.clip(jnp.exp(jax.random.uniform(keys[14], (MECH,), jnp.float32, math.log(0.05), math.log(1.0))), 0.05, 1.0),
    }


courant = 0.25
normal_rows = (1.0, 0.0, 0.0, 1.0, 0.0, 1.0)


def central(padded, along, length):
    def shifted(offset):
        return lax.slice_in_dim(padded, offset, offset + length, axis=along)
    return (8.0 * (shifted(3) - shifted(1)) - (shifted(4) - shifted(0))) / 12.0


def restrict(layer):
    comp_count, x_size, y_size = layer.shape
    return jnp.sum(layer.reshape(comp_count, x_size // 2, 2, y_size // 2, 2), axis=(2, 4)) * 0.25


def prolong(corner_one, right_one, down_one, diagonal):
    comp_count, x_size, y_size = corner_one.shape
    odd_x = 0.5 * (corner_one + right_one)
    odd_y = 0.5 * (corner_one + down_one)
    odd_both = 0.25 * (corner_one + right_one + down_one + diagonal)
    rows_even = jnp.stack([corner_one, odd_x], axis=2).reshape(comp_count, 2 * x_size, y_size)
    rows_odd = jnp.stack([odd_y, odd_both], axis=2).reshape(comp_count, 2 * x_size, y_size)
    return jnp.stack([rows_even, rows_odd], axis=3).reshape(comp_count, 2 * x_size, 2 * y_size)


def fine_vertical(values, beneath):
    levels = values.shape[3]
    ghost_one = 0.5 * (values[:, :, :, levels - 1] + beneath)
    padding = jnp.zeros(values.shape[:3] + (2,), jnp.float32)
    return jnp.concatenate([padding, values, ghost_one[..., None], beneath[..., None]], axis=3)


def coarse_vertical(values, fine_values):
    levels = fine_values.shape[3]
    upper_ghost = restrict(fine_values[:, :, :, levels - 5])
    lower_ghost = restrict(fine_values[:, :, :, levels - 3])
    padding = jnp.zeros(values.shape[:3] + (2,), jnp.float32)
    return jnp.concatenate([upper_ghost[..., None], lower_ghost[..., None], values, padding], axis=3)


def combine_forces(x_part, y_part, z_part):
    force_x = x_part[0] + y_part[0] + z_part[0]
    force_y = x_part[2] + y_part[1] + z_part[1]
    force_z = x_part[1] + y_part[2] + z_part[2]
    return jnp.stack([force_x, force_y, force_z])


def fine_forces(x_padded, y_padded, z_padded, slopes, stretch):
    x_size = y_padded.shape[1]
    y_size = x_padded.shape[2]
    levels = x_padded.shape[3]
    vertical = central(z_padded, 3, levels)
    x_part = central(x_padded, 1, x_size) + slopes[0] * vertical[0:3]
    y_part = central(y_padded, 2, y_size) + slopes[1] * vertical[2:5]
    z_part = stretch * jnp.stack([vertical[1], vertical[4], vertical[5]])
    return combine_forces(x_part, y_part, z_part)


def coarse_forces(x_padded, y_padded, z_padded):
    x_size = y_padded.shape[1]
    y_size = x_padded.shape[2]
    levels = x_padded.shape[3]
    vertical = central(z_padded, 3, levels)
    x_part = 0.5 * central(x_padded, 1, x_size)
    y_part = 0.5 * central(y_padded, 2, y_size)
    z_part = 0.5 * jnp.stack([vertical[1], vertical[4], vertical[5]])
    return combine_forces(x_part, y_part, z_part)


def fine_gradients(x_padded, y_padded, z_padded, slopes, stretch):
    x_size = y_padded.shape[1]
    y_size = x_padded.shape[2]
    levels = x_padded.shape[3]
    vertical = central(z_padded, 3, levels)
    x_grad = central(x_padded, 1, x_size) + slopes[0] * vertical
    y_grad = central(y_padded, 2, y_size) + slopes[1] * vertical
    z_grad = stretch * vertical
    return (x_grad, y_grad, z_grad)


def coarse_gradients(x_padded, y_padded, z_padded):
    x_size = y_padded.shape[1]
    y_size = x_padded.shape[2]
    levels = x_padded.shape[3]
    x_grad = 0.5 * central(x_padded, 1, x_size)
    y_grad = 0.5 * central(y_padded, 2, y_size)
    z_grad = 0.5 * central(z_padded, 3, levels)
    return (x_grad, y_grad, z_grad)


def relax_update(stress, memory, gradients, moduli, anelastic, relax_rates):
    x_grad, y_grad, z_grad = gradients
    strain = courant * jnp.stack([
        x_grad[0],
        0.5 * (z_grad[0] + x_grad[2]),
        0.5 * (y_grad[0] + x_grad[1]),
        y_grad[1],
        0.5 * (z_grad[1] + y_grad[2]),
        z_grad[2]])
    diagonal_rows = jnp.array(normal_rows, jnp.float32)[:, None, None, None]
    dilatation = strain[0] + strain[3] + strain[5]
    lame_first = moduli[0]
    shear_mod = moduli[1]
    bulk_mod = lame_first + (2.0 / 3.0) * shear_mod
    elastic = 2.0 * shear_mod * strain + diagonal_rows * (lame_first * dilatation)
    deviator = strain - diagonal_rows * (dilatation / 3.0)
    target = (2.0 * shear_mod * anelastic[1])[:, None] * deviator[None] + diagonal_rows[None] * (bulk_mod * anelastic[0] * dilatation)[:, None]
    decay_rate = ((1.0 - 0.5 * relax_rates) / (1.0 + 0.5 * relax_rates))[:, None, None, None, None]
    input_gain = (relax_rates / (1.0 + 0.5 * relax_rates))[:, None, None, None, None]
    new_memory = decay_rate * memory + input_gain * target
    new_stress = stress + elastic - 0.5 * jnp.sum(memory + new_memory, axis=0)
    return new_stress, new_memory


def pad_plane(values, along):
    widths = [(0, 0)] * values.ndim
    widths[along] = (2, 2)
    return jnp.pad(values, widths)


def prolong_global(coarse_values):
    layer = jnp.pad(coarse_values[:, :, :, 1], ((0, 0), (0, 1), (0, 1)))
    return prolong(layer[:, :-1, :-1], layer[:, 1:, :-1], layer[:, :-1, 1:], layer[:, 1:, 1:])


def reference(fine_velocity, fine_stress, fine_memory, fine_buoyancy, fine_moduli, fine_anelastic, fine_slopes, fine_stretch, coarse_velocity, coarse_stress, coarse_memory, coarse_buoyancy, coarse_moduli, coarse_anelastic, relax_rates):
    fine_z = fine_vertical(fine_stress, prolong_global(coarse_stress))
    coarse_z = coarse_vertical(coarse_stress, fine_stress)
    fine_push = fine_forces(pad_plane(fine_stress[0:3], 1), pad_plane(fine_stress[2:5], 2), fine_z, fine_slopes, fine_stretch)
    coarse_push = coarse_forces(pad_plane(coarse_stress[0:3], 1), pad_plane(coarse_stress[2:5], 2), coarse_z)
    new_fine_velocity = fine_velocity + (courant * fine_buoyancy) * fine_push
    new_coarse_velocity = coarse_velocity + (courant * coarse_buoyancy) * coarse_push
    fine_z = fine_vertical(new_fine_velocity, prolong_global(new_coarse_velocity))
    coarse_z = coarse_vertical(new_coarse_velocity, new_fine_velocity)
    fine_grads = fine_gradients(pad_plane(new_fine_velocity, 1), pad_plane(new_fine_velocity, 2), fine_z, fine_slopes, fine_stretch)
    coarse_grads = coarse_gradients(pad_plane(new_coarse_velocity, 1), pad_plane(new_coarse_velocity, 2), coarse_z)
    new_fine_stress, new_fine_memory = relax_update(fine_stress, fine_memory, fine_grads, fine_moduli, fine_anelastic, relax_rates)
    new_coarse_stress, new_coarse_memory = relax_update(coarse_stress, coarse_memory, coarse_grads, coarse_moduli, coarse_anelastic, relax_rates)
    return (new_fine_velocity, new_fine_stress, new_fine_memory, new_coarse_velocity, new_coarse_stress, new_coarse_memory)
```

```python
import jax
import jax.numpy as jnp
from jax import lax
from jax.experimental import pallas as pl
from jax.experimental.pallas import tpu as pltpu
from jax.sharding import PartitionSpec as P


courant = 0.25
X_SET = (0, 1, 2)
Y_SET = (2, 3, 4)
Z_SET = (1, 4, 5)
THIN = (0, 1, 5)
f32 = jnp.float32


def rows(shape):
    return lax.broadcasted_iota(jnp.int32, shape, len(shape) - 2)


def lanes(shape):
    return lax.broadcasted_iota(jnp.int32, shape, len(shape) - 1)


def turn(x, k):
    k = k % x.shape[-2]
    return x if k == 0 else pltpu.roll(x, k, x.ndim - 2)


def slide(x, k):
    return pltpu.roll(x, k % x.shape[-1], x.ndim - 1)


def stencil(p2, p1, m1, m2):
    return (2.0 / 3.0) * (p1 - m1) - (1.0 / 12.0) * (p2 - m2)


def along_x(wide):
    n = wide.shape[0] - 4
    return stencil(wide[4 : 4 + n], wide[3 : 3 + n], wide[1 : 1 + n], wide[0:n])


def along_y(f, other):
    r = rows(f.shape)
    n = f.shape[-2]
    p1 = turn(jnp.where(r == 0, other, f), -1)
    p2 = turn(jnp.where(r < 2, other, f), -2)
    m1 = turn(jnp.where(r == n - 1, other, f), 1)
    m2 = turn(jnp.where(r >= n - 2, other, f), 2)
    return stencil(p2, p1, m1, m2)


def along_z(f, above=None, below=None, once=None):
    t = lanes(f.shape)
    n = f.shape[-1]
    if above is None:
        once = slide(f, 1) if once is None else once
        m1 = jnp.where(t == 0, 0.0, once)
        m2 = jnp.where(t < 2, 0.0, slide(f, 2))
    else:
        m1 = slide(jnp.where(t == n - 1, above, f), 1)
        m2 = slide(jnp.where(t >= n - 2, above, f), 2)
    if below is None:
        p1 = jnp.where(t == n - 1, 0.0, slide(f, -1))
        p2 = jnp.where(t >= n - 2, 0.0, slide(f, -2))
    else:
        p1 = slide(jnp.where(t == 0, below, f), -1)
        p2 = slide(jnp.where(t < 2, below, f), -2)
    return stencil(p2, p1, m1, m2)


def along_z_fine(f, prolonged):
    once = slide(f, 1)
    t = lanes(f.shape)
    below = jnp.where(t == 0, 0.5 * (once + slide(prolonged, -1)), prolonged)
    return along_z(f, None, below, once)


def pick_rows(source, table):
    out = None
    r = rows(source[0].shape)
    for row, which, shift in table:
        x = turn(source[which], shift)
        out = x if out is None else jnp.where(r == row, x, out)
    return out


def spread(e):
    u = 0.5 * (e + turn(e, -1))
    r = rows(e.shape)
    even = jnp.where(r < 2, turn(e, -2), jnp.where(r < 4, turn(e, -1), jnp.where(r < 6, e, turn(e, 1))))
    odd = jnp.where(r < 2, turn(u, -1), jnp.where(r < 4, u, jnp.where(r < 6, turn(u, 1), turn(u, 2))))
    return jnp.where(r % 2 == 0, even, odd)


def spread_ring(e):
    u = 0.5 * (e + turn(e, -1))
    r = rows(e.shape)
    return jnp.where(r == 0, turn(e, 2), jnp.where(r < 4, turn(u, 3), jnp.where(r < 7, turn(e, 5), turn(u, 6))))


def widen_planes(q):
    n = q.shape[0] - 1
    mid = 0.5 * (q[0:n] + q[1 : n + 1])
    return jnp.stack([q[0:n], mid], axis=1).reshape((2 * n,) + q.shape[1:])


def ghosts(f):
    n = f.shape[0] // 2
    g = f.reshape((n, 2) + f.shape[1:])
    t = g[:, 0] + g[:, 1]
    t = t + turn(t, -1)
    r = rows(t.shape)
    t = jnp.where(r < 3, turn(t, 2), jnp.where(r == 3, turn(t, 1), jnp.where(r == 4, t, turn(t, -1))))
    last = t.shape[-1] - 1
    return 0.25 * jnp.where(lanes(t.shape) < last, slide(t, 3), slide(t, 2))


def lift(raw):
    return turn(jnp.concatenate([raw, raw], axis=-2), 2)


def vertical_force(d, slope_x, slope_y, stretch):
    return (
        slope_x * d[0] + slope_y * d[2] + stretch * d[1],
        slope_x * d[2] + slope_y * d[3] + stretch * d[4],
        slope_x * d[1] + slope_y * d[4] + stretch * d[5],
    )


def horizontal_force(x_wide, y_pairs):
    dx = [along_x(w) for w in x_wide]
    dy = [along_y(a, b) for a, b in y_pairs]
    return (dx[0] + dy[0], dx[2] + dy[1], dx[1] + dy[2])


def pack_thick(f, low):
    h = f.shape[0] // 2
    a, b = f[0:h], turn(f[h:], 4)
    keep = (rows(a.shape) >= 4) == low
    return jnp.where(keep, a, b), jnp.where(keep, b, a)


def unpack_thick(re, ro, low):
    keep = (rows(re.shape) >= 4) == low
    return jnp.concatenate([jnp.where(keep, ro, re), turn(jnp.where(keep, re, ro), 4)], axis=0)


def pack_thin(f, shift_e, shift_o):
    m = f.shape[0] // 4
    w = [turn(f[j * m : (j + 1) * m], 2 * j) for j in range(4)]
    q = rows(w[0].shape) // 2

    def choose(shift):
        j = lax.rem(q + shift, 4)
        return jnp.where(j == 0, w[0], jnp.where(j == 1, w[1], jnp.where(j == 2, w[2], w[3])))

    return choose(shift_e), choose(shift_o)


def unpack_thin(up, down):
    q = rows(up.shape) // 2
    return jnp.concatenate([turn(jnp.where(q == j, up, down), -2 * j) for j in range(4)], axis=0)


def unpack_thin_coarse(own, up, down):
    n = own.shape[0]
    q = rows(up.shape) // 2
    halo = jnp.stack([turn(jnp.where(q == (1 + x) % 4, up, down), 2 * (2 - x)) for x in range(n)])
    r = rows(own.shape)
    return jnp.where((r >= 2) & (r < 6), own, halo)


def unpack_thick_coarse(own, up, down):
    u, d = turn(up, 6), turn(down, 6)
    u = jnp.concatenate([u, turn(u, 4)], axis=0)
    d = jnp.concatenate([d, turn(d, 4)], axis=0)
    r = rows(own.shape)
    return jnp.where((r >= 2) & (r < 6), own, jnp.where(r >= 6, u, d)), jnp.where(r < 4, u, d)


def coarse_base(fs, cs, cv, cb):
    dz = [along_z(lift(cs[c]), above=ghosts(fs[c]), below=jnp.zeros((1, 1, 1), f32)) for c in Z_SET]
    gain = (0.5 * courant) * lift(cb[...])
    return [lift(cv[c]) + gain * dz[c] for c in range(3)]


def pack_kernel(par, fs, fv, fb, fl, ft, cs, cv, cb, ye, yo, xe, xo, zc):
    low_y = par[0] == 0
    low_x = par[1] == 0
    e_y = jnp.where(low_y, 1, 0)
    at = 0

    def put(e, o):
        nonlocal at
        n = e.shape[0]
        ye[at : at + n] = e
        yo[at : at + n] = o
        at += n

    for c in Y_SET:
        put(*pack_thick(fs[c], low_y))
    for f in [fs[c] for c in THIN] + [fv[c] for c in range(3)] + [fb[...], fl[0], fl[1], ft[...]]:
        put(*pack_thin(f, e_y, 1 - e_y))
    for c in Y_SET:
        raw = cs[c]
        h = raw.shape[0] // 2
        both = jnp.concatenate([raw[0:h], raw[h:]], axis=-2)
        put(both, both)
    base = coarse_base(fs, cs, cv, cb)
    for c in range(3):
        zc[c] = base[c]
    for f in [lift(cs[c]) for c in THIN] + base + [lift(cb[...])]:
        put(*pack_thin(f, 3 - e_y, 2 + e_y))
    nf, nc = fs.shape[1], cs.shape[1]
    for out, high in ((xe, low_x), (xo, jnp.logical_not(low_x))):
        a = jnp.where(high, nf - 2, 0)
        b = jnp.where(high, nc - 2, 0)
        for i, c in enumerate(X_SET):
            out[2 * i : 2 * i + 2] = fs[c, pl.ds(a, 2)]
        for c in range(6):
            out[6 + c, 0:4] = cs[c, b]
            out[6 + c, 4:8] = cs[c, b + 1]


class Arrived:
    def __init__(self, par, ye, yo, nf, nc):
        self.low = par[0] == 0
        self.ye, self.yo, self.nf, self.nc = ye, yo, nf, nc
        h, m = nf // 2, nf // 4
        self.thick = {c: i * h for i, c in enumerate(Y_SET)}
        at = 3 * h
        self.thin = {}
        for name in ("s0", "s1", "s5", "v0", "v1", "v2", "b", "l0", "l1", "t"):
            self.thin[name] = at
            at += m
        g = nc // 2
        self.cthick = {c: at + i * g for i, c in enumerate(Y_SET)}
        at += 3 * g
        self.cthin = {}
        for name in ("s0", "s1", "s5", "z0", "z1", "z2", "b"):
            self.cthin[name] = at
            at += nc // 4

    def sides(self, at, n):
        e, o = self.ye[at : at + n], self.yo[at : at + n]
        return jnp.where(self.low, e, o), jnp.where(self.low, o, e)

    def ring(self, name):
        if name in ("s2", "s3", "s4"):
            at, n = self.thick[int(name[1])], self.nf // 2
            return unpack_thick(self.ye[at : at + n], self.yo[at : at + n], self.low)
        return unpack_thin(*self.sides(self.thin[name], self.nf // 4))

    def wide(self, name, own):
        if name in ("s2", "s3", "s4"):
            up, down = self.sides(self.cthick[int(name[1])], self.nc // 2)
            return unpack_thick_coarse(own, up, down)
        up, down = self.sides(self.cthin[name], self.nc // 4)
        return unpack_thin_coarse(own, up[0], down[0]), None


def x_sides(par, xe, xo, at, n):
    low = par[1] == 0
    e, o = xe[at : at + n], xo[at : at + n]
    return jnp.where(low, e, o), jnp.where(low, o, e)


def coarse_stress_wide(arrived, cs):
    return [arrived.wide("s%d" % c, lift(cs[c])) for c in range(6)]


def coarse_motion(arrived, zc, cb, wide, x_wide):
    gain = (0.5 * courant) * arrived.wide("b", lift(cb[...]))[0]
    force = horizontal_force(x_wide, [wide[c] for c in Y_SET])
    return [arrived.wide("z%d" % c, zc[c])[0] + gain * force[c] for c in range(3)]


def own_rows(x):
    r = rows(x.shape)
    return jnp.where((r >= 2) & (r < 6), x, 0.0)


def velocity_kernel(par, fs, fv, fb, fl, ft, cs, cb, zc, ye, yo, xe, xo, vf, vc, x2e, x2o):
    nf, nc = fs.shape[1], cs.shape[1]
    arrived = Arrived(par, ye, yo, nf, nc)
    wide = coarse_stress_wide(arrived, cs)
    ring = {c: arrived.ring("s%d" % c) for c in range(5)}

    right, left, cright, cleft = [], [], [], []
    for i, c in enumerate(X_SET):
        p, m = x_sides(par, xe, xo, 2 * i, 2)
        right.append(p)
        left.append(m)
    for c in range(6):
        p, m = x_sides(par, xe, xo, 6 + c, 1)
        cright.append(own_rows(jnp.concatenate([turn(p, 2), turn(p, 6)], axis=0)))
        cleft.append(own_rows(jnp.concatenate([turn(m, 2), turn(m, 6)], axis=0)))

    x_wide = [jnp.concatenate([cleft[c], wide[c][0], cright[c]], axis=0) for c in X_SET]
    moved = coarse_motion(arrived, zc, cb, wide, x_wide)
    for c in range(3):
        vc[c] = moved[c]

    x_fine = [jnp.concatenate([left[i], fs[c], right[i]], axis=0) for i, c in enumerate(X_SET)]
    side = horizontal_force(x_fine, [(fs[c], ring[c]) for c in Y_SET])
    dz = []
    for c in range(6):
        q = spread(jnp.concatenate([wide[c][0], cright[c][0:1]], axis=0))
        dz.append(along_z_fine(fs[c], widen_planes(q)))
    down = vertical_force(dz, fl[0], fl[1], ft[...])
    gain = courant * fb[...]
    for c in range(3):
        vf[c] = fv[c] + gain * (side[c] + down[c])

    low_x = par[1] == 0
    base_b = arrived.wide("b", lift(cb[...]))[0]
    for out, high in ((x2e, low_x), (x2o, jnp.logical_not(low_x))):
        a = jnp.where(high, nf - 2, 0)
        at = 0
        for c in range(3):
            out[at : at + 2] = vf[c, pl.ds(a, 2)]
            at += 2
        for c in X_SET:
            out[at : at + 2] = jnp.where(high, ring[c][nf - 2 :], ring[c][0:2])
            at += 2
        for c in range(3):
            out[at : at + 2] = jnp.where(high, moved[c][nc - 2 :], moved[c][0:2])
            at += 2
        for c in X_SET:
            out[at : at + 2] = jnp.where(high, wide[c][0][nc - 2 :], wide[c][0][0:2])
            at += 2
        for c in (3, 4, 5):
            out[at : at + 1] = wide[c][0][0:1]
            at += 1
        out[at : at + 1] = base_b[0:1]
        at += 1
        for f in (fb[nf - 1], fl[0, nf - 1], fl[1, nf - 1], ft[nf - 1]):
            out[at] = f
            at += 1


def relax(stress, memory, grads, lame, shear, anelastic, rates, new_stress, new_memory, cut):
    gx, gy, gz = grads
    strain = [
        courant * gx[0],
        (0.5 * courant) * (gz[0] + gx[2]),
        (0.5 * courant) * (gy[0] + gx[1]),
        courant * gy[1],
        (0.5 * courant) * (gz[1] + gy[2]),
        courant * gz[2],
    ]
    theta = strain[0] + strain[3] + strain[5]
    twice = 2.0 * shear
    bulk = (lame + (2.0 / 3.0) * shear) * theta
    third = theta * (1.0 / 3.0)
    press = lame * theta
    total = [None] * 6
    for l in range(memory.shape[0]):
        w = jnp.full((1, 1, 128), rates[l], f32)
        inv = 1.0 / (1.0 + 0.5 * w)
        decay, gain = (1.0 - 0.5 * w) * inv, w * inv
        shear_part = gain * (twice * cut(anelastic, 1, l))
        bulk_part = gain * (bulk * cut(anelastic, 0, l))
        for c in range(6):
            old = cut(memory, l, c)
            if c in (0, 3, 5):
                new = decay * old + (shear_part * (strain[c] - third) + bulk_part)
            else:
                new = decay * old + shear_part * strain[c]
            new_memory(l, c, new)
            both = old + new
            total[c] = both if total[c] is None else total[c] + both
    for c in range(6):
        elastic = twice * strain[c]
        if c in (0, 3, 5):
            elastic = elastic + press
        new_stress(c, cut(stress, c) + elastic - 0.5 * total[c])


def final_kernel(par, rates, fs, fm, fb, fmod, fan, fl, ft, cs, cm, cb, cmod, can, zc, ye, yo, xe, xo, x2e, x2o, vf, vc, ofv, ofs, ofm, ocv, ocs, ocm):
    nf, nc = fs.shape[1], cs.shape[1]
    arrived = Arrived(par, ye, yo, nf, nc)
    wide = coarse_stress_wide(arrived, cs)
    ring = [arrived.ring("s%d" % c) for c in range(6)]
    at = 0

    def take(n):
        nonlocal at
        p, m = x_sides(par, x2e, x2o, at, n)
        at += n
        return p, m

    motion_x = [take(2) for _ in range(3)]
    ring_x = [take(2) for _ in X_SET]
    cmotion_x = [take(2) for _ in range(3)]
    cstress_x = [take(2) for _ in X_SET]
    corner = [cstress_x[c][0][0:1] for c in X_SET] + [take(1)[0] for _ in range(3)]
    corner_b = take(1)[0]
    edge_b, edge_lx, edge_ly, edge_t = (take(1)[1] for _ in range(4))

    def column_fix(g, b, lx, ly, t):
        r, zero = rows(b.shape), jnp.zeros(b.shape, f32)
        d = [along_z_fine(zero, 0.25 * turn(x, 1)) for x in g]
        force = vertical_force(d, lx, ly, t)
        return [jnp.where(r == b.shape[-2] - 1, courant * b * f, 0.0) for f in force]

    own_fix = column_fix(corner, fb[nf - 1 : nf], fl[0, nf - 1 : nf], fl[1, nf - 1 : nf], ft[nf - 1 : nf])
    left_fix = column_fix([wide[c][0][0:1] for c in range(6)], edge_b, edge_lx, edge_ly, edge_t)

    own = [jnp.concatenate([vf[c, 0 : nf - 1], vf[c, nf - 1 : nf] + own_fix[c]], axis=0) for c in range(3)]
    for c in range(3):
        ofv[c] = own[c]
    q_planes = [jnp.concatenate([wide[c][0], corner[c]], axis=0) for c in range(6)]
    dz = [along_z_fine(ring[c], widen_planes(spread_ring(q_planes[c]))) for c in range(6)]
    down = vertical_force(dz, arrived.ring("l0"), arrived.ring("l1"), arrived.ring("t"))
    x_ring = [jnp.concatenate([ring_x[i][1], ring[c], ring_x[i][0]], axis=0) for i, c in enumerate(X_SET)]
    side = horizontal_force(x_ring, [(ring[c], fs[c]) for c in Y_SET])
    gain = courant * arrived.ring("b")
    beyond = [arrived.ring("v%d" % c) + gain * (side[c] + down[c]) for c in range(3)]

    cx = [jnp.concatenate([cstress_x[c][1], wide[c][0], cstress_x[c][0]], axis=0) for c in X_SET]
    cmoved = coarse_motion(arrived, zc, cb, wide, cx)
    for c in range(3):
        ocv[c] = cmoved[c][:, 2:6]
    gain = (0.5 * courant) * corner_b
    r = rows(corner_b.shape)
    after = []
    for c, s in enumerate((0, 2, 1)):
        near = wide[s][0][nc - 2 :]
        fix = gain * ((1.0 / 12.0) * near[0:1] - (2.0 / 3.0) * near[1:2])
        after.append(cmotion_x[c][0][0:1] + jnp.where(r == 6, fix, 0.0))

    gx, gy, gz = [], [], []
    for c in range(3):
        p, m = motion_x[c]
        m = jnp.concatenate([m[0:1], m[1:2] + left_fix[c]], axis=0)
        q = spread(jnp.concatenate([cmoved[c], after[c]], axis=0))
        d = along_z_fine(own[c], widen_planes(q))
        gx.append(along_x(jnp.concatenate([m, own[c], p], axis=0)) + fl[0] * d)
        gy.append(along_y(own[c], beyond[c]) + fl[1] * d)
        gz.append(ft[...] * d)

    def set_fs(c, x):
        ofs[c] = x

    def set_fm(l, c, x):
        ofm[l, c] = x

    relax(fs, fm, (gx, gy, gz), fmod[0], fmod[1], fan, rates, set_fs, set_fm, lambda ref, *i: ref[i])

    gx, gy, gz = [], [], []
    for c in range(3):
        p, m = cmotion_x[c]
        d = along_z(cmoved[c], above=ghosts(own[c]), below=jnp.zeros((1, 1, 1), f32))
        gx.append(0.5 * along_x(jnp.concatenate([m, cmoved[c], p], axis=0)))
        gy.append(0.5 * along_y(cmoved[c], cmoved[c]))
        gz.append(0.5 * d)

    def set_cs(c, x):
        ocs[c] = x[:, 2:6]

    def set_cm(l, c, x):
        ocm[l, c] = x[:, 2:6]

    relax(cs, cm, (gx, gy, gz), lift(cmod[0]), lift(cmod[1]), can, rates, set_cs, set_cm, lambda ref, *i: lift(ref[i]))


def swap(values, axis, first):
    count = lax.axis_size(axis)
    pairs = []
    for i in range(first, count - 1, 2):
        pairs += [(i, i + 1), (i + 1, i)]
    return lax.ppermute(values, axis, pairs)


def call(kernel, outs, name, cost, scalars, *args):
    vmem = pl.BlockSpec(memory_space=pltpu.VMEM)
    smem = pl.BlockSpec(memory_space=pltpu.SMEM)
    return pl.pallas_call(
        kernel,
        out_shape=[jax.ShapeDtypeStruct(s, f32) for s in outs],
        in_specs=[smem] * len(scalars) + [vmem] * len(args),
        out_specs=[vmem] * len(outs),
        name=name,
        cost_estimate=pl.CostEstimate(flops=cost, bytes_accessed=cost, transcendentals=0),
    )(*scalars, *args)


def local(fv, fs, fm, fb, fmod, fan, fl, ft, cv, cs, cm, cb, cmod, can, rates):
    nf, rows_f, nz = fs.shape[1:]
    nc, rows_c = cs.shape[1:3]
    par = jnp.stack([lax.axis_index("gy") % 2, lax.axis_index("gx") % 2]).astype(jnp.int32)
    tile = (rows_f, nz)
    y_tiles = 3 * (nf // 2) + 10 * (nf // 4) + 3 * (nc // 2) + 7 * (nc // 4)
    x_tiles = 12
    x2_tiles = 32
    ye, yo, xe, xo, zc = call(
        pack_kernel,
        [(y_tiles,) + tile] * 2 + [(x_tiles,) + tile] * 2 + [(3, nc) + tile],
        "pack", 1000000, [par], fs, fv, fb, fl, ft, cs, cv, cb,
    )
    ye = swap(ye, "gy", 0)
    yo = swap(yo, "gy", 1)
    xo = swap(xo, "gx", 1)
    xe = swap(xe, "gx", 0)
    vf, vc, x2e, x2o = call(
        velocity_kernel,
        [fv.shape, (3, nc) + tile] + [(x2_tiles,) + tile] * 2,
        "velocity", 1000000, [par], fs, fv, fb, fl, ft, cs, cb, zc, ye, yo, xe, xo,
    )
    x2o = swap(x2o, "gx", 1)
    x2e = swap(x2e, "gx", 0)
    return tuple(call(
        final_kernel,
        [fv.shape, fs.shape, fm.shape, cv.shape, cs.shape, cm.shape],
        "strain", 2000000, [par, rates], fs, fm, fb, fmod, fan, fl, ft, cs, cm, cb, cmod, can, zc, ye, yo, xe, xo, x2e, x2o, vf, vc,
    ))


def solution(mesh):
    placed = (
        P(None, "gx", "gy", None),
        P(None, "gx", "gy", None),
        P(None, None, "gx", "gy", None),
        P("gx", "gy", None),
        P(None, "gx", "gy", None),
        P(None, None, "gx", "gy", None),
        P(None, "gx", "gy", None),
        P("gx", "gy", None),
        P(None, "gx", "gy", None),
        P(None, "gx", "gy", None),
        P(None, None, "gx", "gy", None),
        P("gx", "gy", None),
        P(None, "gx", "gy", None),
        P(None, None, "gx", "gy", None),
        P(),
    )
    out = P(None, "gx", "gy", None)
    deep = P(None, None, "gx", "gy", None)
    return jax.shard_map(
        local,
        mesh=mesh,
        in_specs=placed,
        out_specs=(out, out, deep, out, out, deep),
        check_vma=False,
    )
```

```python
import jax
import jax.numpy as jnp
from jax import lax
from jax.experimental import pallas as pl
from jax.experimental.pallas import tpu as pltpu
from jax.sharding import PartitionSpec as P


courant = 0.25
X_SET = (0, 1, 2)
Y_SET = (2, 3, 4)
Z_SET = (1, 4, 5)
THIN = (0, 1, 5)
f32 = jnp.float32


def rows(shape):
    return lax.broadcasted_iota(jnp.int32, shape, len(shape) - 2)


def lanes(shape):
    return lax.broadcasted_iota(jnp.int32, shape, len(shape) - 1)


def turn(x, k):
    k = k % x.shape[-2]
    return x if k == 0 else pltpu.roll(x, k, x.ndim - 2)


def slide(x, k):
    return pltpu.roll(x, k % x.shape[-1], x.ndim - 1)


def stencil(p2, p1, m1, m2):
    return (2.0 / 3.0) * (p1 - m1) - (1.0 / 12.0) * (p2 - m2)


def along_x(wide):
    n = wide.shape[0] - 4
    return stencil(wide[4 : 4 + n], wide[3 : 3 + n], wide[1 : 1 + n], wide[0:n])


def along_y(f, other):
    r = rows(f.shape)
    n = f.shape[-2]
    p1 = turn(jnp.where(r == 0, other, f), -1)
    p2 = turn(jnp.where(r < 2, other, f), -2)
    m1 = turn(jnp.where(r == n - 1, other, f), 1)
    m2 = turn(jnp.where(r >= n - 2, other, f), 2)
    return stencil(p2, p1, m1, m2)


def along_z(f, above=None, below=None, once=None):
    t = lanes(f.shape)
    n = f.shape[-1]
    if above is None:
        once = slide(f, 1) if once is None else once
        m1 = jnp.where(t == 0, 0.0, once)
        m2 = jnp.where(t < 2, 0.0, slide(f, 2))
    else:
        m1 = slide(jnp.where(t == n - 1, above, f), 1)
        m2 = slide(jnp.where(t >= n - 2, above, f), 2)
    if below is None:
        p1 = jnp.where(t == n - 1, 0.0, slide(f, -1))
        p2 = jnp.where(t >= n - 2, 0.0, slide(f, -2))
    else:
        p1 = slide(jnp.where(t == 0, below, f), -1)
        p2 = slide(jnp.where(t < 2, below, f), -2)
    return stencil(p2, p1, m1, m2)


def along_z_fine(f, prolonged):
    once = slide(f, 1)
    t = lanes(f.shape)
    below = jnp.where(t == 0, 0.5 * (once + slide(prolonged, -1)), prolonged)
    return along_z(f, None, below, once)


def pick_rows(source, table):
    out = None
    r = rows(source[0].shape)
    for row, which, shift in table:
        x = turn(source[which], shift)
        out = x if out is None else jnp.where(r == row, x, out)
    return out


def spread(e):
    u = 0.5 * (e + turn(e, -1))
    r = rows(e.shape)
    even = jnp.where(r < 2, turn(e, -2), jnp.where(r < 4, turn(e, -1), jnp.where(r < 6, e, turn(e, 1))))
    odd = jnp.where(r < 2, turn(u, -1), jnp.where(r < 4, u, jnp.where(r < 6, turn(u, 1), turn(u, 2))))
    return jnp.where(r % 2 == 0, even, odd)


def spread_ring(e):
    u = 0.5 * (e + turn(e, -1))
    r = rows(e.shape)
    return jnp.where(r == 0, turn(e, 2), jnp.where(r < 4, turn(u, 3), jnp.where(r < 7, turn(e, 5), turn(u, 6))))


def widen_planes(q):
    n = q.shape[0] - 1
    mid = 0.5 * (q[0:n] + q[1 : n + 1])
    return jnp.stack([q[0:n], mid], axis=1).reshape((2 * n,) + q.shape[1:])


def ghosts(f):
    n = f.shape[0] // 2
    g = f.reshape((n, 2) + f.shape[1:])
    t = g[:, 0] + g[:, 1]
    t = t + turn(t, -1)
    r = rows(t.shape)
    t = jnp.where(r < 3, turn(t, 2), jnp.where(r == 3, turn(t, 1), jnp.where(r == 4, t, turn(t, -1))))
    last = t.shape[-1] - 1
    return 0.25 * jnp.where(lanes(t.shape) < last, slide(t, 3), slide(t, 2))


def lift(raw):
    return turn(jnp.concatenate([raw, raw], axis=-2), 2)


def vertical_force(d, slope_x, slope_y, stretch):
    return (
        slope_x * d[0] + slope_y * d[2] + stretch * d[1],
        slope_x * d[2] + slope_y * d[3] + stretch * d[4],
        slope_x * d[1] + slope_y * d[4] + stretch * d[5],
    )


def horizontal_force(x_wide, y_pairs):
    dx = [along_x(w) for w in x_wide]
    dy = [along_y(a, b) for a, b in y_pairs]
    return (dx[0] + dy[0], dx[2] + dy[1], dx[1] + dy[2])


def pack_thick(f, low):
    h = f.shape[0] // 2
    a, b = f[0:h], turn(f[h:], 4)
    keep = (rows(a.shape) >= 4) == low
    return jnp.where(keep, a, b), jnp.where(keep, b, a)


def unpack_thick(re, ro, low):
    keep = (rows(re.shape) >= 4) == low
    return jnp.concatenate([jnp.where(keep, ro, re), turn(jnp.where(keep, re, ro), 4)], axis=0)


def pack_thin(f, shift_e, shift_o):
    m = f.shape[0] // 4
    w = [turn(f[j * m : (j + 1) * m], 2 * j) for j in range(4)]
    q = rows(w[0].shape) // 2

    def choose(shift):
        j = lax.rem(q + shift, 4)
        return jnp.where(j == 0, w[0], jnp.where(j == 1, w[1], jnp.where(j == 2, w[2], w[3])))

    return choose(shift_e), choose(shift_o)


def unpack_thin(up, down):
    q = rows(up.shape) // 2
    return jnp.concatenate([turn(jnp.where(q == j, up, down), -2 * j) for j in range(4)], axis=0)


def unpack_thin_coarse(own, up, down):
    n = own.shape[0]
    q = rows(up.shape) // 2
    halo = jnp.stack([turn(jnp.where(q == (1 + x) % 4, up, down), 2 * (2 - x)) for x in range(n)])
    r = rows(own.shape)
    return jnp.where((r >= 2) & (r < 6), own, halo)


def unpack_thick_coarse(own, up, down):
    u, d = turn(up, 6), turn(down, 6)
    u = jnp.concatenate([u, turn(u, 4)], axis=0)
    d = jnp.concatenate([d, turn(d, 4)], axis=0)
    r = rows(own.shape)
    return jnp.where((r >= 2) & (r < 6), own, jnp.where(r >= 6, u, d)), jnp.where(r < 4, u, d)


def coarse_base(fs, cs, cv, cb):
    dz = [along_z(lift(cs[c]), above=ghosts(fs[c]), below=jnp.zeros((1, 1, 1), f32)) for c in Z_SET]
    gain = (0.5 * courant) * lift(cb[...])
    return [lift(cv[c]) + gain * dz[c] for c in range(3)]


def parities():
    return [lax.rem(lax.axis_index(a), 2) for a in ("gy", "gx")]


def pack_kernel(hfs, hfv, hfb, hfl, hft, hcs, hcv, hcb, hrates, fs, fv, fb, fl, ft, cs, cb, speed, ye, yo, xe, xo, zc, cv, rates, sem):
    par = parities()
    moves = {}
    for i, (name, src, dst) in enumerate((
        ("fs", hfs, fs), ("cs", hcs, cs), ("fv", hfv, fv), ("fb", hfb, fb), ("fl", hfl, fl),
        ("ft", hft, ft), ("cv", hcv, cv), ("cb", hcb, cb), ("rates", hrates, rates),
    )):
        moves[name] = pltpu.make_async_copy(src, dst, sem.at[i])
        moves[name].start()
    low_y = par[0] == 0
    low_x = par[1] == 0
    e_y = jnp.where(low_y, 1, 0)
    at = 0

    def put(e, o):
        nonlocal at
        n = e.shape[0]
        ye[at : at + n] = e
        yo[at : at + n] = o
        at += n

    def thin(f):
        put(*pack_thin(f, e_y, 1 - e_y))

    moves["fs"].wait()
    for c in Y_SET:
        put(*pack_thick(fs[c], low_y))
    for c in THIN:
        thin(fs[c])
    moves["cs"].wait()
    nf, nc = fs.shape[1], cs.shape[1]
    for out, high in ((xe, low_x), (xo, jnp.logical_not(low_x))):
        a = jnp.where(high, nf - 2, 0)
        b = jnp.where(high, nc - 2, 0)
        for i, c in enumerate(X_SET):
            out[2 * i : 2 * i + 2] = fs[c, pl.ds(a, 2)]
        for c in range(6):
            out[6 + c, 0:4] = cs[c, b]
            out[6 + c, 4:8] = cs[c, b + 1]
    for name in ("fv", "fb", "fl", "ft", "cv", "cb", "rates"):
        moves[name].wait()
    for f in [fv[c] for c in range(3)] + [fb[...], fl[0], fl[1], ft[...]]:
        thin(f)
    for c in Y_SET:
        raw = cs[c]
        h = raw.shape[0] // 2
        both = jnp.concatenate([raw[0:h], raw[h:]], axis=-2)
        put(both, both)
    base = coarse_base(fs, cs, cv, cb)
    for c in range(3):
        zc[c] = base[c]
    for f in [lift(cs[c]) for c in THIN] + base + [lift(cb[...])]:
        put(*pack_thin(f, 3 - e_y, 2 + e_y))
    for l in range(rates.shape[0]):
        w = jnp.full(speed.shape[1:], rates[l], f32)
        speed[l] = w


class Arrived:
    def __init__(self, par, ye, yo, nf, nc):
        self.low = par[0] == 0
        self.ye, self.yo, self.nf, self.nc = ye, yo, nf, nc
        h, m = nf // 2, nf // 4
        self.thick = {c: i * h for i, c in enumerate(Y_SET)}
        at = 3 * h
        self.thin = {}
        for name in ("s0", "s1", "s5", "v0", "v1", "v2", "b", "l0", "l1", "t"):
            self.thin[name] = at
            at += m
        g = nc // 2
        self.cthick = {c: at + i * g for i, c in enumerate(Y_SET)}
        at += 3 * g
        self.cthin = {}
        for name in ("s0", "s1", "s5", "z0", "z1", "z2", "b"):
            self.cthin[name] = at
            at += nc // 4

    def sides(self, at, n):
        e, o = self.ye[at : at + n], self.yo[at : at + n]
        return jnp.where(self.low, e, o), jnp.where(self.low, o, e)

    def ring(self, name):
        if name in ("s2", "s3", "s4"):
            at, n = self.thick[int(name[1])], self.nf // 2
            return unpack_thick(self.ye[at : at + n], self.yo[at : at + n], self.low)
        return unpack_thin(*self.sides(self.thin[name], self.nf // 4))

    def wide(self, name, own):
        if name in ("s2", "s3", "s4"):
            up, down = self.sides(self.cthick[int(name[1])], self.nc // 2)
            return unpack_thick_coarse(own, up, down)
        up, down = self.sides(self.cthin[name], self.nc // 4)
        return unpack_thin_coarse(own, up[0], down[0]), None


def x_sides(par, xe, xo, at, n):
    low = par[1] == 0
    e, o = xe[at : at + n], xo[at : at + n]
    return jnp.where(low, e, o), jnp.where(low, o, e)


def coarse_stress_wide(arrived, cs):
    return [arrived.wide("s%d" % c, lift(cs[c])) for c in range(6)]


def coarse_motion(arrived, zc, cb, wide, x_wide):
    gain = (0.5 * courant) * arrived.wide("b", lift(cb[...]))[0]
    force = horizontal_force(x_wide, [wide[c] for c in Y_SET])
    return [arrived.wide("z%d" % c, zc[c])[0] + gain * force[c] for c in range(3)]


def own_rows(x):
    r = rows(x.shape)
    return jnp.where((r >= 2) & (r < 6), x, 0.0)


def inner(shape):
    r = rows(shape)
    return (r >= 2) & (r < 6)


def merge_outer(a, b):
    return jnp.where(inner(a.shape), turn(b, 4), a)


def merge_inner(a, b):
    return jnp.where(inner(a.shape), a, turn(b, 4))


def single_rows(pairs):
    r = rows(pairs[0][0].shape)
    out = None
    for i, (x, row) in enumerate(pairs):
        x = turn(x, 7 - i - row)
        out = x if out is None else jnp.where(r == 7 - i, x, out)
    return out


def beside(par, xe, xo):
    right, left = [], []
    for c in range(6):
        p, m = x_sides(par, xe, xo, 6 + c, 1)
        right.append(own_rows(jnp.concatenate([turn(p, 2), turn(p, 6)], axis=0)))
        left.append(own_rows(jnp.concatenate([turn(m, 2), turn(m, 6)], axis=0)))
    return right, left


def velocity_kernel(fs, fv, fb, fl, ft, cs, cb, zc, ye, yo, xe, xo, vf, x2e, x2o):
    par = parities()
    nf, nc = fs.shape[1], cs.shape[1]
    arrived = Arrived(par, ye, yo, nf, nc)
    wide = coarse_stress_wide(arrived, cs)
    ring = {c: arrived.ring("s%d" % c) for c in range(5)}

    right, left = [], []
    for i, c in enumerate(X_SET):
        p, m = x_sides(par, xe, xo, 2 * i, 2)
        right.append(p)
        left.append(m)
    cright, cleft = beside(par, xe, xo)

    x_wide = [jnp.concatenate([cleft[c], wide[c][0], cright[c]], axis=0) for c in X_SET]
    moved = coarse_motion(arrived, zc, cb, wide, x_wide)
    x_fine = [jnp.concatenate([left[i], fs[c], right[i]], axis=0) for i, c in enumerate(X_SET)]
    side = horizontal_force(x_fine, [(fs[c], ring[c]) for c in Y_SET])
    dz = []
    for c in range(6):
        q = spread(jnp.concatenate([wide[c][0], cright[c][0:1]], axis=0))
        dz.append(along_z_fine(fs[c], widen_planes(q)))
    down = vertical_force(dz, fl[0], fl[1], ft[...])
    gain = courant * fb[...]
    for c in range(3):
        vf[c] = fv[c] + gain * (side[c] + down[c])

    low_x = par[1] == 0
    base_b = arrived.wide("b", lift(cb[...]))[0]
    edge = single_rows([(fb[nf - 1], 7), (fl[0, nf - 1], 7), (fl[1, nf - 1], 7), (ft[nf - 1], 7)] + [(moved[c][0], 6) for c in range(3)])
    for out, high in ((x2e, low_x), (x2o, jnp.logical_not(low_x))):
        a = jnp.where(high, nf - 2, 0)
        at = 0
        for c in range(3):
            out[at : at + 2] = vf[c, pl.ds(a, 2)]
            at += 2

        def ends(f):
            n = f.shape[0]
            return jnp.where(high, f[n - 2], f[0]), jnp.where(high, f[n - 1], f[1])

        for c in X_SET:
            out[at] = merge_outer(*ends(ring[c]))
            at += 1
        for c in range(3):
            out[at] = merge_inner(*ends(moved[c]))
            at += 1
        for c in X_SET:
            out[at] = merge_outer(*ends(wide[c][0]))
            at += 1
        out[at] = merge_outer(wide[3][0][0], wide[4][0][0])
        out[at + 1] = merge_outer(wide[5][0][0], base_b[0])
        out[at + 2] = edge


def relax(stress, memory, grads, lame, shear, anelastic, rates, new_stress, new_memory, done_memory, cut):
    gx, gy, gz = grads
    strain = [
        courant * gx[0],
        (0.5 * courant) * (gz[0] + gx[2]),
        (0.5 * courant) * (gy[0] + gx[1]),
        courant * gy[1],
        (0.5 * courant) * (gz[1] + gy[2]),
        courant * gz[2],
    ]
    theta = strain[0] + strain[3] + strain[5]
    twice = 2.0 * shear
    bulk = (lame + (2.0 / 3.0) * shear) * theta
    third = theta * (1.0 / 3.0)
    press = lame * theta
    total = [None] * 6
    for l in range(memory.shape[0]):
        w = rates[l : l + 1]
        inv = 1.0 / (1.0 + 0.5 * w)
        decay, gain = (1.0 - 0.5 * w) * inv, w * inv
        shear_part = gain * (twice * cut(anelastic, 1, l))
        bulk_part = gain * (bulk * cut(anelastic, 0, l))
        for c in range(6):
            old = cut(memory, l, c)
            if c in (0, 3, 5):
                new = decay * old + (shear_part * (strain[c] - third) + bulk_part)
            else:
                new = decay * old + shear_part * strain[c]
            new_memory(l, c, new)
            both = old + new
            total[c] = both if total[c] is None else total[c] + both
        done_memory(l)
    for c in range(6):
        elastic = twice * strain[c]
        if c in (0, 3, 5):
            elastic = elastic + press
        new_stress(c, cut(stress, c) + elastic - 0.5 * total[c])


def final_kernel(fs, fm, fb, fmod, fan, fl, ft, cs, cm, cb, cmod, can, rates, zc, ye, yo, xe, xo, x2e, x2o, vf, hfv, hfs, hfm, hcv, hcs, hcm, ofv, ofs, ofm, ocv, ocs, ocm, sem):
    par = parities()
    sent = []

    def send(src, dst):
        move = pltpu.make_async_copy(src, dst, sem.at[len(sent)])
        move.start()
        sent.append(move)

    nf, nc = fs.shape[1], cs.shape[1]
    arrived = Arrived(par, ye, yo, nf, nc)
    wide = coarse_stress_wide(arrived, cs)
    ring = [arrived.ring("s%d" % c) for c in range(6)]
    at = 0

    def take(n):
        nonlocal at
        p, m = x_sides(par, x2e, x2o, at, n)
        at += n
        return p, m

    def two(x):
        return jnp.concatenate([x, turn(x, 4)], axis=0)

    motion_x = [take(2) for _ in range(3)]
    ring_x = [[two(x) for x in take(1)] for _ in X_SET]
    cmotion_x = [[two(x) for x in take(1)] for _ in range(3)]
    near = beside(par, xe, xo)

    def fill(x, own):
        return jnp.where(inner(x.shape), own, x)

    cstress_x = [[fill(two(x), side[c]) for x, side in zip(take(1), near)] for c in X_SET]
    pair_a, pair_b = take(1)[0], take(1)[0]
    corner = [cstress_x[c][0][0:1] for c in X_SET]
    corner += [fill(x, near[0][3 + i][0:1]) for i, x in enumerate((pair_a, turn(pair_a, 4), pair_b))]
    corner_b = turn(pair_b, 4)
    edge_p, edge_m = take(1)
    edge_b, edge_lx, edge_ly, edge_t = (turn(edge_m, i) for i in range(4))
    edge_v = [turn(edge_p, 3 + i) for i in range(3)]

    def column_fix(g, b, lx, ly, t):
        r, zero = rows(b.shape), jnp.zeros(b.shape, f32)
        d = [along_z_fine(zero, 0.25 * turn(x, 1)) for x in g]
        force = vertical_force(d, lx, ly, t)
        return [jnp.where(r == b.shape[-2] - 1, courant * b * f, 0.0) for f in force]

    own_fix = column_fix(corner, fb[nf - 1 : nf], fl[0, nf - 1 : nf], fl[1, nf - 1 : nf], ft[nf - 1 : nf])
    left_fix = column_fix([wide[c][0][0:1] for c in range(6)], edge_b, edge_lx, edge_ly, edge_t)

    own = [jnp.concatenate([vf[c, 0 : nf - 1], vf[c, nf - 1 : nf] + own_fix[c]], axis=0) for c in range(3)]
    for c in range(3):
        ofv[c] = own[c]
    send(ofv, hfv)
    q_planes = [jnp.concatenate([wide[c][0], corner[c]], axis=0) for c in range(6)]
    dz = [along_z_fine(ring[c], widen_planes(spread_ring(q_planes[c]))) for c in range(6)]
    down = vertical_force(dz, arrived.ring("l0"), arrived.ring("l1"), arrived.ring("t"))
    x_ring = [jnp.concatenate([ring_x[i][1], ring[c], ring_x[i][0]], axis=0) for i, c in enumerate(X_SET)]
    side = horizontal_force(x_ring, [(ring[c], fs[c]) for c in Y_SET])
    gain = courant * arrived.ring("b")
    beyond = [arrived.ring("v%d" % c) + gain * (side[c] + down[c]) for c in range(3)]

    cx = [jnp.concatenate([cstress_x[c][1], wide[c][0], cstress_x[c][0]], axis=0) for c in X_SET]
    cmoved = coarse_motion(arrived, zc, cb, wide, cx)
    for c in range(3):
        ocv[c] = cmoved[c][:, 2:6]
    send(ocv, hcv)
    gain = (0.5 * courant) * corner_b
    r = rows(corner_b.shape)
    after = []
    for c, s in enumerate((0, 2, 1)):
        last = wide[s][0][nc - 2 :]
        fix = gain * ((1.0 / 12.0) * last[0:1] - (2.0 / 3.0) * last[1:2])
        after.append(jnp.where(r == 6, edge_v[c] + fix, cmotion_x[c][0][0:1]))

    gx, gy, gz = [], [], []
    for c in range(3):
        p, m = motion_x[c]
        m = jnp.concatenate([m[0:1], m[1:2] + left_fix[c]], axis=0)
        q = spread(jnp.concatenate([cmoved[c], after[c]], axis=0))
        d = along_z_fine(own[c], widen_planes(q))
        gx.append(along_x(jnp.concatenate([m, own[c], p], axis=0)) + fl[0] * d)
        gy.append(along_y(own[c], beyond[c]) + fl[1] * d)
        gz.append(ft[...] * d)

    def set_fs(c, x):
        ofs[c] = x

    def set_fm(l, c, x):
        ofm[l, c] = x

    relax(fs, fm, (gx, gy, gz), fmod[0], fmod[1], fan, rates, set_fs, set_fm, lambda l: send(ofm.at[l], hfm.at[l]), lambda ref, *i: ref[i])
    send(ofs, hfs)

    gx, gy, gz = [], [], []
    for c in range(3):
        p, m = cmotion_x[c]
        d = along_z(cmoved[c], above=ghosts(own[c]), below=jnp.zeros((1, 1, 1), f32))
        gx.append(0.5 * along_x(jnp.concatenate([m, cmoved[c], p], axis=0)))
        gy.append(0.5 * along_y(cmoved[c], cmoved[c]))
        gz.append(0.5 * d)

    def set_cs(c, x):
        ocs[c] = x[:, 2:6]

    def set_cm(l, c, x):
        ocm[l, c] = x[:, 2:6]

    relax(cs, cm, (gx, gy, gz), lift(cmod[0]), lift(cmod[1]), can, rates, set_cs, set_cm, lambda l: send(ocm.at[l], hcm.at[l]), lambda ref, *i: lift(ref[i]))
    send(ocs, hcs)
    for move in sent:
        move.wait()


def swap(values, axis, first):
    count = lax.axis_size(axis)
    pairs = []
    for i in range(first, count - 1, 2):
        pairs += [(i, i + 1), (i + 1, i)]
    return lax.ppermute(values, axis, pairs)


def call(kernel, outs, name, cost, args, hbm_in=False, hbm_out=False, scratch=()):
    vmem = pl.BlockSpec(memory_space=pltpu.VMEM)
    hbm = pl.BlockSpec(memory_space=pltpu.HBM)
    if hbm_in:
        args = [pltpu.with_memory_space_constraint(x, pltpu.HBM) for x in args]
    return pl.pallas_call(
        kernel,
        out_shape=[jax.ShapeDtypeStruct(s, f32) for s in outs],
        in_specs=[hbm if hbm_in else vmem] * len(args),
        out_specs=[hbm if hbm_out else vmem] * len(outs),
        scratch_shapes=scratch,
        name=name,
        compiler_params=pltpu.CompilerParams(vmem_limit_bytes=16 << 20),
        cost_estimate=pl.CostEstimate(flops=cost, bytes_accessed=cost, transcendentals=0),
    )(*args)


def local(fv, fs, fm, fb, fmod, fan, fl, ft, cv, cs, cm, cb, cmod, can, rates):
    nf, rows_f, nz = fs.shape[1:]
    nc = cs.shape[1]
    tile = (rows_f, nz)
    mechs = rates.shape[0]
    y_tiles = 3 * (nf // 2) + 10 * (nf // 4) + 3 * (nc // 2) + 7 * (nc // 4)
    x_tiles = 12
    x2_tiles = 18
    shapes = [x.shape for x in (fs, fv, fb, fl, ft, cs, cb)]
    *kept, ye, yo, xe, xo, zc = call(
        pack_kernel,
        shapes + [(mechs,) + tile] + [(y_tiles,) + tile] * 2 + [(x_tiles,) + tile] * 2 + [(3, nc) + tile],
        "pack", 1000000, [fs, fv, fb, fl, ft, cs, cv, cb, rates], hbm_in=True,
        scratch=[pltpu.VMEM(cv.shape, f32), pltpu.SMEM(rates.shape, f32), pltpu.SemaphoreType.DMA((9,))],
    )
    fs, fv, fb, fl, ft, cs, cb, speed = kept
    ye = swap(ye, "gy", 0)
    yo = swap(yo, "gy", 1)
    xo = swap(xo, "gx", 1)
    xe = swap(xe, "gx", 0)
    vf, x2e, x2o = call(
        velocity_kernel,
        [fv.shape] + [(x2_tiles,) + tile] * 2,
        "velocity", 1000000, [fs, fv, fb, fl, ft, cs, cb, zc, ye, yo, xe, xo],
    )
    x2o = swap(x2o, "gx", 1)
    x2e = swap(x2e, "gx", 0)
    shapes = [x.shape for x in (fv, fs, fm, cv, cs, cm)]
    return tuple(call(
        final_kernel,
        shapes,
        "strain", 2000000,
        [fs, fm, fb, fmod, fan, fl, ft, cs, cm, cb, cmod, can, speed, zc, ye, yo, xe, xo, x2e, x2o, vf],
        hbm_out=True,
        scratch=[pltpu.VMEM(x, f32) for x in shapes] + [pltpu.SemaphoreType.DMA((4 + 2 * mechs,))],
    ))


def solution(mesh):
    placed = (
        P(None, "gx", "gy", None),
        P(None, "gx", "gy", None),
        P(None, None, "gx", "gy", None),
        P("gx", "gy", None),
        P(None, "gx", "gy", None),
        P(None, None, "gx", "gy", None),
        P(None, "gx", "gy", None),
        P("gx", "gy", None),
        P(None, "gx", "gy", None),
        P(None, "gx", "gy", None),
        P(None, None, "gx", "gy", None),
        P("gx", "gy", None),
        P(None, "gx", "gy", None),
        P(None, None, "gx", "gy", None),
        P(),
    )
    out = P(None, "gx", "gy", None)
    deep = P(None, None, "gx", "gy", None)
    return jax.shard_map(
        local,
        mesh=mesh,
        in_specs=placed,
        out_specs=(out, out, deep, out, out, deep),
        check_vma=False,
    )
```
